32 devices in a mesh: row: 4 (over x, core), col: 8 (over z, y).
Axes of the slice: x: 2, y: 2, z: 4, core: 2. Of those that a mesh axis runs over, the one named last changes fastest.
Arguments:
- video: float32 [1, 128, 64, 64, 256], P(None, 'row', 'col'), may hold values from -6 to 6
- decay_rates: float32 [3, 256, 64], replicated, may hold values from 0.5 to 4
- frequencies: float32 [3, 256, 64], replicated, may hold values from 0 to 64
- input_vec: float32 [3, 2, 256, 64], replicated, may hold values from -6 to 6
- output_vec: float32 [3, 2, 256, 64], replicated, may hold values from -3 to 3
- lowrank_vec: float32 [3, 2, 256, 64], replicated, may hold values from -3 to 3
- step_scale: float32 [3, 256], replicated, may hold values from 0.5 to 8
- skip_gain: float32 [256], replicated, may hold values from -4 to 4
Outputs:
- layer_out: float32 [1, 128, 64, 64, 256], P(None, 'row', 'col')
The draws below stay inside these ranges and needn't reach their ends.
All inputs are finite; a program needn't handle non-finite values.
Results may differ from the reference program's by a relative error of at most 0.000076.
Values sent between devices are 32-bit elements; how exact they have to be, the bound alone decides.
No kernel may reach another device: no remote copies, remote signals or barrier semaphores. Data moves between devices by JAX's collectives and lax.ppermute only.
A program may use at most 192 MiB of HBM per device.

```python
import math
import jax
import jax.numpy as jnp
from jax import lax

CLIPS = 1
FRAMES = 128
HEIGHT = 64
WIDTH = 64
CH = 256
STATES = 64


def levels(own_key, shape, pieces, smallest, largest):
    def one(axis_at, shards_of):
        draws = jax.random.uniform(jax.random.fold_in(jax.random.fold_in(own_key, 6), axis_at), (shards_of,), jnp.float32, smallest / len(pieces), largest / len(pieces))
        return jnp.repeat(jnp.exp(draws), shape[axis_at] // shards_of).reshape((-1,) + (1,) * (len(shape) - axis_at - 1))

    loudness = one(*pieces[0])
    for cut in pieces[1:]:
        loudness = loudness * one(*cut)
    return loudness


def normal_values(stream_key, dims, deviation, bound, cuts=(), held_as=jnp.bfloat16):
    values = jax.random.normal(stream_key, dims, jnp.float32) * deviation
    if len(cuts) > 0:
        values = levels(stream_key, dims, cuts, -0.22, 0.18) * values
    return jnp.clip(values, min=-bound, max=bound).astype(held_as)


def setup_inputs(seed: int = 0) -> dict:
    key_of = jax.random.split(jax.random.key(seed), 9)
    return {
        "video": normal_values(key_of[0], (CLIPS, FRAMES, HEIGHT, WIDTH, CH), 1.0, 6.0, ((1, 4), (2, 8)), jnp.float32),
        "decay_rates": jnp.clip(jnp.exp(jax.random.uniform(key_of[1], (3, CH, STATES), jnp.float32, math.log(0.5), math.log(4.0))), 0.5, 4.0),
        "frequencies": jnp.clip(jax.random.uniform(key_of[2], (3, CH, STATES), jnp.float32, 0.0, 64.0), 0.0, 64.0),
        "input_vec": normal_values(key_of[3], (3, 2, CH, STATES), 1.0, 6.0, (), jnp.float32),
        "output_vec": normal_values(key_of[4], (3, 2, CH, STATES), 0.5, 3.0, (), jnp.float32),
        "lowrank_vec": normal_values(key_of[5], (3, 2, CH, STATES), 0.5, 3.0, (), jnp.float32),
        "step_scale": jnp.clip(jnp.exp(jax.random.uniform(key_of[6], (3, CH), jnp.float32, math.log(0.5), math.log(8.0))), 0.5, 8.0),
        "skip_gain": normal_values(key_of[7], (CH,), 1.0, 4.0, (), jnp.float32),
    }


def axis_kernel(decay, oscill, input_part, output_part, lowrank_part, scales, length):
    step_size = scales / length
    index = jnp.arange(length)
    angles = 2.0 * jnp.pi * index.astype(decay.dtype) / length
    unit_root = jnp.exp(-1j * angles)
    eigen = -decay + 1j * oscill
    denominator = (2.0 / step_size)[:, None, None] * (1.0 - unit_root)[None, :, None] - eigen[:, None, :] * (1.0 + unit_root)[None, :, None]
    in_vec = input_part[0] + 1j * input_part[1]
    out_vec = output_part[0] + 1j * output_part[1]
    low_vec = lowrank_part[0] + 1j * lowrank_part[1]
    cauchy_cb = jnp.sum((out_vec * in_vec)[:, None, :] / denominator, -1)
    cauchy_cp = jnp.sum((out_vec * low_vec)[:, None, :] / denominator, -1)
    cauchy_pb = jnp.sum((jnp.conj(low_vec) * in_vec)[:, None, :] / denominator, -1)
    cauchy_pp = jnp.sum((jnp.conj(low_vec) * low_vec)[:, None, :] / denominator, -1)
    shifted = (1.0 + unit_root)[None, :]
    generating = 2.0 * (cauchy_cb - shifted * cauchy_cp * cauchy_pb / (1.0 + shifted * cauchy_pp))
    return jnp.real(jnp.fft.ifft(generating, axis=1)).T


def reference(video, decay_rates, frequencies, input_vec, output_vec, lowrank_vec, step_scale, skip_gain):
    lengths = (FRAMES, HEIGHT, WIDTH)
    kernels = [axis_kernel(decay_rates[axis_num], frequencies[axis_num], input_vec[axis_num], output_vec[axis_num], lowrank_vec[axis_num], step_scale[axis_num], lengths[axis_num]) for axis_num in range(3)]
    time_spec = jnp.fft.fft(kernels[0], n=2 * FRAMES, axis=0)
    height_spec = jnp.fft.fft(kernels[1], axis=0)
    width_spec = jnp.fft.fft(kernels[2], axis=0)
    group_size = 16
    groups = CH // group_size

    def filter_group(operands):
        group_video, group_time, group_height, group_width = operands
        spectrum = jnp.fft.fftn(group_video, s=(2 * FRAMES, HEIGHT, WIDTH), axes=(1, 2, 3))
        spectrum = spectrum * group_time[None, :, None, None, :] * group_height[None, None, :, None, :] * group_width[None, None, None, :, :]
        return jnp.real(jnp.fft.ifftn(spectrum, axes=(1, 2, 3)))[:, :FRAMES]

    grouped = jnp.moveaxis(video.reshape(CLIPS, FRAMES, HEIGHT, WIDTH, groups, group_size), 4, 0)

    def regroup(spec):
        return jnp.moveaxis(spec.reshape(spec.shape[0], groups, group_size), 1, 0)

    filtered = lax.map(filter_group, (grouped, regroup(time_spec), regroup(height_spec), regroup(width_spec)))
    filtered = jnp.moveaxis(filtered, 0, 4).reshape(CLIPS, FRAMES, HEIGHT, WIDTH, CH)
    return jax.nn.gelu(filtered + skip_gain * video, approximate=False)
```

```python
import functools
import math

import jax
import jax.numpy as jnp
from jax import lax
from jax.experimental import pallas as pl
from jax.experimental.pallas import tpu as pltpu
from jax.sharding import PartitionSpec as P

full_precision = lax.Precision.HIGHEST
LANES = 128
SUBLANES = 8
CHUNKS = 2


def complex_mul(left_re, left_im, right_re, right_im):
    return (left_re * right_re - left_im * right_im, left_re * right_im + left_im * right_re)


def complex_div(left_re, left_im, right_re, right_im):
    magnitude = right_re * right_re + right_im * right_im
    return (
        (left_re * right_re + left_im * right_im) / magnitude,
        (left_im * right_re - left_re * right_im) / magnitude,
    )


def cauchy_sum(num_re, num_im, inv_re, inv_im):
    num_re, num_im = num_re[:, None, :], num_im[:, None, :]
    return (
        jnp.sum(num_re * inv_re - num_im * inv_im, -1),
        jnp.sum(num_re * inv_im + num_im * inv_re, -1),
    )


def axis_rows(decay, oscill, input_part, output_part, lowrank_part, scales, length, lags):
    step_size = scales / length
    two_over = (2.0 / step_size)[:, None, None]
    index = jnp.arange(length, dtype=jnp.int32)
    angles = 2.0 * math.pi / length * index.astype(jnp.float32)
    cosine = jnp.cos(angles)
    sine_vals = jnp.sin(angles)
    minus_cos = (1.0 - cosine)[None, :, None]
    plus_cos = (1.0 + cosine)[None, :, None]
    sine_col = sine_vals[None, :, None]
    den_re = two_over * minus_cos + decay[:, None, :] * plus_cos - oscill[:, None, :] * sine_col
    den_im = two_over * sine_col - decay[:, None, :] * sine_col - oscill[:, None, :] * plus_cos
    magnitude = den_re * den_re + den_im * den_im
    inv_re = den_re / magnitude
    inv_im = -den_im / magnitude
    prod_cb = complex_mul(output_part[0], output_part[1], input_part[0], input_part[1])
    prod_cp = complex_mul(output_part[0], output_part[1], lowrank_part[0], lowrank_part[1])
    prod_pb = complex_mul(lowrank_part[0], -lowrank_part[1], input_part[0], input_part[1])
    prod_pp = lowrank_part[0] * lowrank_part[0] + lowrank_part[1] * lowrank_part[1]
    cauchy_cb = cauchy_sum(prod_cb[0], prod_cb[1], inv_re, inv_im)
    cauchy_cp = cauchy_sum(prod_cp[0], prod_cp[1], inv_re, inv_im)
    cauchy_pb = cauchy_sum(prod_pb[0], prod_pb[1], inv_re, inv_im)
    cauchy_pp = cauchy_sum(prod_pp, jnp.zeros_like(prod_pp), inv_re, inv_im)
    shift_re = (1.0 + cosine)[None, :]
    shift_im = (-sine_vals)[None, :]
    cross_re, cross_im = complex_mul(cauchy_cp[0], cauchy_cp[1], cauchy_pb[0], cauchy_pb[1])
    cross_re, cross_im = complex_mul(shift_re, shift_im, cross_re, cross_im)
    lower_re, lower_im = complex_mul(shift_re, shift_im, cauchy_pp[0], cauchy_pp[1])
    quot_re, quot_im = complex_div(cross_re, cross_im, 1.0 + lower_re, lower_im)
    gen_re = 2.0 * (cauchy_cb[0] - quot_re)
    gen_im = 2.0 * (cauchy_cb[1] - quot_im)
    table = index[:, None] * (lags % length)[None, :] % length
    table = 2.0 * math.pi / length * table.astype(jnp.float32)
    rows = jnp.dot(gen_re, jnp.cos(table), precision=full_precision) - jnp.dot(
        gen_im, jnp.sin(table), precision=full_precision
    )
    return rows / length


def pack_kernel(frames, pack, src_ref, dst_ref):
    flat = dst_ref.reshape(LANES * frames, LANES)

    @pl.loop(0, frames, unroll=2)
    def _(step):
        tile = src_ref[step].reshape(LANES, LANES)
        flat[pl.ds(step, LANES, stride=frames), :] = tile.T


def pack_chunk(video, chunk, pack):
    frames, height, width, _ = video.shape
    pairs = height // pack
    return pl.pallas_call(
        functools.partial(pack_kernel, frames, pack),
        grid=(pairs,),
        in_specs=[pl.BlockSpec((frames, pack, width, LANES), lambda i: (0, i, 0, chunk))],
        out_specs=pl.BlockSpec((LANES, 1, frames, LANES), lambda i: (0, i, 0, 0)),
        out_shape=jax.ShapeDtypeStruct((LANES, pairs, frames, LANES), jnp.float32),
        cost_estimate=pl.CostEstimate(
            flops=0, transcendentals=0, bytes_accessed=8 * frames * height * width * LANES
        ),
        name="pack",
    )(video)


def unpack_kernel(frames, pack, src_ref, *refs):
    dst_ref = refs[-1]
    flat = src_ref.reshape(LANES * frames, LANES)
    width = LANES // pack

    @pl.loop(0, frames, unroll=2)
    def _(step):
        tile = flat[pl.ds(step, LANES, stride=frames), :]
        dst_ref[step] = tile.T.reshape(pack, width, LANES)


def unpack_chunk(packed, chunk, pack, shape, into):
    frames, height, width, _ = shape
    pairs = height // pack
    in_specs = [pl.BlockSpec((LANES, 1, frames, LANES), lambda i: (0, i, 0, 0))]
    operands = [packed]
    aliases = {}
    if into is not None:
        in_specs.append(pl.BlockSpec(memory_space=pl.ANY))
        operands.append(into)
        aliases = {1: 0}
    return pl.pallas_call(
        functools.partial(unpack_kernel, frames, pack),
        grid=(pairs,),
        in_specs=in_specs,
        out_specs=pl.BlockSpec((frames, pack, width, LANES), lambda i: (0, i, 0, chunk)),
        out_shape=jax.ShapeDtypeStruct(shape, jnp.float32),
        input_output_aliases=aliases,
        cost_estimate=pl.CostEstimate(
            flops=0, transcendentals=0, bytes_accessed=8 * frames * height * width * LANES
        ),
        name="unpack",
    )(*operands)


def split(value):
    high = value.astype(jnp.bfloat16)
    low = (value - high.astype(jnp.float32)).astype(jnp.bfloat16)
    return high, low


def shifted_rows(row, count):
    return pltpu.roll(jnp.broadcast_to(row, (count, LANES)), 0, 1, stride=1, stride_axis=0)


def dot(left, right):
    return jnp.dot(left, right, preferred_element_type=jnp.float32)


def left_stack(matrix):
    high, low = split(matrix)
    return jnp.concatenate(
        [
            jnp.concatenate([high, high], 1),
            jnp.concatenate([low, jnp.zeros_like(low)], 1),
        ],
        0,
    )


def conv_kernel(dims, taps_ref, src_ref, dst_ref, work):
    row_count, col_count, pairs, frame_rows, pack = dims
    frames = row_count * frame_rows
    quads = col_count * pairs
    width = LANES // pack
    taps = taps_ref[0]

    time_i = lax.broadcasted_iota(jnp.int32, (frames, frames), 0)
    time_j = lax.broadcasted_iota(jnp.int32, (frames, frames), 1)
    time_mat = jnp.where(time_i >= time_j, shifted_rows(taps[0:1], frames)[:, :frames], 0.0)
    time_stack = left_stack(time_mat)

    cell_i = lax.broadcasted_iota(jnp.int32, (LANES, LANES), 0)
    cell_j = lax.broadcasted_iota(jnp.int32, (LANES, LANES), 1)
    width_mat = jnp.where(cell_i // width == cell_j // width, shifted_rows(taps[1:2], LANES), 0.0)
    width_high, width_low = split(width_mat)
    width_stack = jnp.concatenate(
        [
            jnp.concatenate([width_high, width_low], 1),
            jnp.concatenate([width_high, jnp.zeros_like(width_low)], 1),
        ],
        0,
    )

    def load(quad):
        col = quad // pairs
        first = pl.multiple_of(quad % pairs * frame_rows, frame_rows)
        return jnp.concatenate(
            [
                src_ref[row, col, 0, pl.ds(first, frame_rows), :]
                for row in range(row_count)
            ],
            0,
        )

    @pl.loop(0, quads // 2)
    def _(step):
        both = jnp.concatenate([load(2 * step), load(2 * step + 1)], 1)
        high, low = split(both)
        conv = dot(time_stack, jnp.concatenate([high, low], 0))
        conv = conv[:frames] + conv[frames:]
        conv = jnp.concatenate([conv[:, :LANES], conv[:, LANES:]], 0)
        high, low = split(conv)
        conv = dot(jnp.concatenate([high, low], 1), width_stack)
        conv = conv[:, :LANES] + conv[:, LANES:]
        work[pl.ds(pl.multiple_of(2 * frames * step, 2 * frames), 2 * frames), :] = conv

    height_stack = jnp.concatenate(
        [left_stack(shifted_rows(taps[2 + e : 3 + e], quads)[:, :quads]) for e in range(3)], 0
    )
    group = 4
    lane = lax.broadcasted_iota(jnp.int32, (quads, group * LANES), 1) % LANES

    @pl.loop(0, frames // group)
    def _(step):
        tiles = [
            work[pl.ds(group * step + e, quads, stride=frames), :] for e in range(group)
        ]
        high, low = split(jnp.concatenate(tiles, 1))
        conv = dot(height_stack, jnp.concatenate([high, low], 0))
        same = conv[:quads] + conv[quads : 2 * quads]
        upper = conv[2 * quads : 3 * quads] + conv[3 * quads : 4 * quads]
        lower = conv[4 * quads : 5 * quads] + conv[5 * quads :]
        cross = jnp.where(lane < width, upper, lower)
        for e in range(group):
            cols = slice(e * LANES, (e + 1) * LANES)
            work[pl.ds(group * step + e, quads, stride=frames), :] = same[:, cols] + pltpu.roll(
                cross[:, cols], width, 1
            )

    gain = taps[5:6]

    @pl.loop(0, quads)
    def _(quad):
        col = quad // pairs
        first = pl.multiple_of(quad % pairs * frame_rows, frame_rows)
        for row in range(row_count):
            start = pl.multiple_of(quad * frames + row * frame_rows, frame_rows)
            value = work[pl.ds(start, frame_rows), :]
            value = value + gain * src_ref[row, col, 0, pl.ds(first, frame_rows), :]
            value = 0.5 * value * (1.0 + lax.erf(value * math.sqrt(0.5)))
            dst_ref[row, col, 0, pl.ds(first, frame_rows), :] = value


def conv_chunk(packed, taps, row_count, col_count, pairs, frame_rows, pack):
    share = packed.shape[2]
    rows = packed.shape[3]
    frames = row_count * frame_rows
    quads = col_count * pairs
    block = pl.BlockSpec((row_count, col_count, 1, rows, LANES), lambda i: (0, 0, i, 0, 0))
    cells = frames * quads * LANES
    return pl.pallas_call(
        functools.partial(conv_kernel, (row_count, col_count, pairs, frame_rows, pack)),
        grid=(share,),
        in_specs=[pl.BlockSpec((1, SUBLANES, LANES), lambda i: (i, 0, 0)), block],
        out_specs=block,
        out_shape=jax.ShapeDtypeStruct(packed.shape, jnp.float32),
        scratch_shapes=[pltpu.VMEM((quads * frames, LANES), jnp.float32)],
        cost_estimate=pl.CostEstimate(
            flops=share * cells * 2000, transcendentals=share * cells, bytes_accessed=8 * share * cells
        ),
        name="conv",
    )(taps, packed)


def on_device(
    video, decay_rates, frequencies, input_vec, output_vec, lowrank_vec, step_scale, skip_gain
):
    clip_count, frame_rows, height_rows, width_cells, channels = video.shape
    row_count = lax.axis_size("row")
    col_count = lax.axis_size("col")
    frames = frame_rows * row_count
    height = height_rows * col_count
    dev_count = row_count * col_count
    pack = LANES // width_cells
    pairs = height_rows // pack
    chunk_width = channels // CHUNKS
    share = chunk_width // dev_count
    assert clip_count == 1 and pack == 2 and chunk_width == LANES and frames == LANES
    me = lax.axis_index("row") * col_count + lax.axis_index("col")
    shape = video.shape[1:]
    video = video.reshape(shape)

    def own(array, dim):
        split_shape = array.shape[:dim] + (CHUNKS, chunk_width) + array.shape[dim + 1 :]
        part = lax.dynamic_slice_in_dim(array.reshape(split_shape), me * share, share, dim + 1)
        return part.reshape(array.shape[:dim] + (CHUNKS * share,) + array.shape[dim + 1 :])

    def everyone(first):
        return [
            lax.all_to_all(e, ("row", "col"), split_axis=0, concat_axis=0, tiled=True)
            for e in first
        ]

    packed = [pack_chunk(video, chunk, pack) for chunk in range(CHUNKS)]
    packed = everyone(packed)

    decay_rates, frequencies = own(decay_rates, 1), own(frequencies, 1)
    input_vec, output_vec, lowrank_vec = own(input_vec, 2), own(output_vec, 2), own(lowrank_vec, 2)
    step_scale, gains = own(step_scale, 1), own(skip_gain, 0)
    lane = jnp.arange(LANES, dtype=jnp.int32)
    lags = (
        -lane,
        jnp.concatenate([-pack * lane, 1 - pack * lane, -1 - pack * lane]),
        lane,
    )
    time_rows, height_rows_taps, width_rows = (
        axis_rows(
            decay_rates[axis],
            frequencies[axis],
            input_vec[axis],
            output_vec[axis],
            lowrank_vec[axis],
            step_scale[axis],
            length,
            lags[axis],
        )
        for axis, length in enumerate((frames, height, width_cells))
    )
    own_count = CHUNKS * share
    taps = jnp.concatenate(
        [
            time_rows[:, None],
            width_rows[:, None],
            height_rows_taps.reshape(own_count, 3, LANES),
            jnp.broadcast_to(gains[:, None, None], (own_count, SUBLANES - 5, LANES)),
        ],
        1,
    ).reshape(CHUNKS, share, SUBLANES, LANES)

    outs = []
    for chunk in range(CHUNKS):
        block = packed[chunk].reshape(row_count, col_count, share, pairs * frame_rows, LANES)
        block = conv_chunk(block, taps[chunk], row_count, col_count, pairs, frame_rows, pack)
        outs.append(block.reshape(LANES, pairs, frame_rows, LANES))
    outs = everyone(outs)
    result = None
    for chunk in range(CHUNKS):
        result = unpack_chunk(outs[chunk], chunk, pack, shape, result)
    return result.reshape((clip_count,) + shape)


def solution(mesh):
    in_specs = (P(None, "row", "col", None, None), P(), P(), P(), P(), P(), P(), P())
    out_specs = P(None, "row", "col", None, None)
    return jax.shard_map(
        on_device, mesh=mesh, in_specs=in_specs, out_specs=out_specs, check_vma=False
    )
```

```python
import functools
import math

import jax
import jax.numpy as jnp
from jax import lax
from jax.experimental import pallas as pl
from jax.experimental.pallas import tpu as pltpu
from jax.sharding import PartitionSpec as P

full_precision = lax.Precision.HIGHEST
LANES = 128
SUBLANES = 8
CHUNKS = 2
MOST_PERMUTES = 32


def complex_mul(left_re, left_im, right_re, right_im):
    return (left_re * right_re - left_im * right_im, left_re * right_im + left_im * right_re)


def complex_div(left_re, left_im, right_re, right_im):
    magnitude = right_re * right_re + right_im * right_im
    return (
        (left_re * right_re + left_im * right_im) / magnitude,
        (left_im * right_re - left_re * right_im) / magnitude,
    )


def cauchy_sum(num_re, num_im, inv_re, inv_im):
    num_re, num_im = num_re[:, None, :], num_im[:, None, :]
    return (
        jnp.sum(num_re * inv_re - num_im * inv_im, -1),
        jnp.sum(num_re * inv_im + num_im * inv_re, -1),
    )


def axis_rows(decay, oscill, input_part, output_part, lowrank_part, scales, length, lags):
    step_size = scales / length
    two_over = (2.0 / step_size)[:, None, None]
    index = jnp.arange(length, dtype=jnp.int32)
    angles = 2.0 * math.pi / length * index.astype(jnp.float32)
    cosine = jnp.cos(angles)
    sine_vals = jnp.sin(angles)
    minus_cos = (1.0 - cosine)[None, :, None]
    plus_cos = (1.0 + cosine)[None, :, None]
    sine_col = sine_vals[None, :, None]
    den_re = two_over * minus_cos + decay[:, None, :] * plus_cos - oscill[:, None, :] * sine_col
    den_im = two_over * sine_col - decay[:, None, :] * sine_col - oscill[:, None, :] * plus_cos
    magnitude = den_re * den_re + den_im * den_im
    inv_re = den_re / magnitude
    inv_im = -den_im / magnitude
    prod_cb = complex_mul(output_part[0], output_part[1], input_part[0], input_part[1])
    prod_cp = complex_mul(output_part[0], output_part[1], lowrank_part[0], lowrank_part[1])
    prod_pb = complex_mul(lowrank_part[0], -lowrank_part[1], input_part[0], input_part[1])
    prod_pp = lowrank_part[0] * lowrank_part[0] + lowrank_part[1] * lowrank_part[1]
    cauchy_cb = cauchy_sum(prod_cb[0], prod_cb[1], inv_re, inv_im)
    cauchy_cp = cauchy_sum(prod_cp[0], prod_cp[1], inv_re, inv_im)
    cauchy_pb = cauchy_sum(prod_pb[0], prod_pb[1], inv_re, inv_im)
    cauchy_pp = cauchy_sum(prod_pp, jnp.zeros_like(prod_pp), inv_re, inv_im)
    shift_re = (1.0 + cosine)[None, :]
    shift_im = (-sine_vals)[None, :]
    cross_re, cross_im = complex_mul(cauchy_cp[0], cauchy_cp[1], cauchy_pb[0], cauchy_pb[1])
    cross_re, cross_im = complex_mul(shift_re, shift_im, cross_re, cross_im)
    lower_re, lower_im = complex_mul(shift_re, shift_im, cauchy_pp[0], cauchy_pp[1])
    quot_re, quot_im = complex_div(cross_re, cross_im, 1.0 + lower_re, lower_im)
    gen_re = 2.0 * (cauchy_cb[0] - quot_re)
    gen_im = 2.0 * (cauchy_cb[1] - quot_im)
    table = index[:, None] * (lags % length)[None, :] % length
    table = 2.0 * math.pi / length * table.astype(jnp.float32)
    rows = jnp.dot(gen_re, jnp.cos(table), precision=full_precision) - jnp.dot(
        gen_im, jnp.sin(table), precision=full_precision
    )
    return rows / length


def pack_kernel(frames, share, me_ref, src_ref, *refs):
    dst_refs, flat = refs[:-1], refs[-1]
    pitch = frames + 1

    @pl.loop(0, frames, unroll=4)
    def _(step):
        tile = src_ref[step].reshape(LANES, LANES)
        flat[pl.ds(step, LANES, stride=pitch), :] = tile.T

    for place, dst_ref in enumerate(dst_refs):
        first = (me_ref[0] ^ place) * share
        for e in range(share):
            dst_ref[e, 0] = flat[pl.ds((first + e) * pitch, frames), :]


def pack_chunk(video, me, chunk, pack, devices):
    frames, height, width, _ = video.shape
    pairs = height // pack
    share = LANES // devices
    block = pl.BlockSpec((share, 1, frames, LANES), lambda i, me: (0, i, 0, 0))
    return pl.pallas_call(
        functools.partial(pack_kernel, frames, share),
        grid_spec=pltpu.PrefetchScalarGridSpec(
            num_scalar_prefetch=1,
            grid=(pairs,),
            in_specs=[pl.BlockSpec((frames, pack, width, LANES), lambda i, me: (0, i, 0, chunk))],
            out_specs=[block] * devices,
            scratch_shapes=[pltpu.VMEM((LANES * (frames + 1), LANES), jnp.float32)],
        ),
        out_shape=[jax.ShapeDtypeStruct((share, pairs, frames, LANES), jnp.float32)] * devices,
        cost_estimate=pl.CostEstimate(
            flops=0, transcendentals=0, bytes_accessed=8 * frames * height * width * LANES
        ),
        name="pack",
    )(me, video)


def unpack_kernel(frames, pack, share, devices, me_ref, *refs):
    src_refs, dst_ref, flat = refs[:devices], refs[-2], refs[-1]
    width = LANES // pack
    pitch = frames + 1
    for place, src_ref in enumerate(src_refs):
        first = (me_ref[0] ^ place) * share
        for e in range(share):
            flat[pl.ds((first + e) * pitch, frames), :] = src_ref[e, 0]

    @pl.loop(0, frames, unroll=4)
    def _(step):
        tile = flat[pl.ds(step, LANES, stride=pitch), :]
        dst_ref[step] = tile.T.reshape(pack, width, LANES)


def unpack_chunk(packed, me, chunk, pack, shape, into):
    frames, height, width, _ = shape
    pairs = height // pack
    devices = len(packed)
    share = LANES // devices
    in_specs = [pl.BlockSpec((share, 1, frames, LANES), lambda i, me: (0, i, 0, 0))] * devices
    operands = list(packed)
    aliases = {}
    if into is not None:
        in_specs.append(pl.BlockSpec(memory_space=pl.ANY))
        operands.append(into)
        aliases = {1 + devices: 0}
    return pl.pallas_call(
        functools.partial(unpack_kernel, frames, pack, share, devices),
        grid_spec=pltpu.PrefetchScalarGridSpec(
            num_scalar_prefetch=1,
            grid=(pairs,),
            in_specs=in_specs,
            out_specs=pl.BlockSpec((frames, pack, width, LANES), lambda i, me: (0, i, 0, chunk)),
            scratch_shapes=[pltpu.VMEM((LANES * (frames + 1), LANES), jnp.float32)],
        ),
        out_shape=jax.ShapeDtypeStruct(shape, jnp.float32),
        input_output_aliases=aliases,
        cost_estimate=pl.CostEstimate(
            flops=0, transcendentals=0, bytes_accessed=8 * frames * height * width * LANES
        ),
        name="unpack",
    )(me, *operands)


def split(value):
    high = value.astype(jnp.bfloat16)
    low = (value - high.astype(jnp.float32)).astype(jnp.bfloat16)
    return high, low


def shifted_rows(row, count):
    return pltpu.roll(jnp.broadcast_to(row, (count, LANES)), 0, 1, stride=1, stride_axis=0)


def dot(left, right):
    return jnp.dot(left, right, preferred_element_type=jnp.float32)


def left_stack(matrix):
    high, low = split(matrix)
    return jnp.concatenate(
        [
            jnp.concatenate([high, high], 1),
            jnp.concatenate([low, low], 1),
        ],
        0,
    )


def conv_kernel(dims, me_ref, taps_ref, *refs):
    row_count, col_count, pairs, frame_rows, pack = dims
    devices = row_count * col_count
    src_refs, dst_refs = refs[:devices], refs[devices : 2 * devices]
    held, work = refs[2 * devices :]
    frames = row_count * frame_rows
    pitch = frames + 1
    quads = col_count * pairs
    width = LANES // pack
    taps = taps_ref[0]

    for place, src_ref in enumerate(src_refs):
        held[me_ref[0] ^ place] = src_ref[0]

    time_i = lax.broadcasted_iota(jnp.int32, (frames, frames), 0)
    time_j = lax.broadcasted_iota(jnp.int32, (frames, frames), 1)
    time_mat = jnp.where(time_i >= time_j, shifted_rows(taps[0:1], frames)[:, :frames], 0.0)
    time_stack = left_stack(time_mat)

    cell_i = lax.broadcasted_iota(jnp.int32, (LANES, LANES), 0)
    cell_j = lax.broadcasted_iota(jnp.int32, (LANES, LANES), 1)
    width_mat = jnp.where(cell_i // width == cell_j // width, shifted_rows(taps[1:2], LANES), 0.0)
    width_high, width_low = split(width_mat)
    width_stack = jnp.concatenate(
        [
            jnp.concatenate([width_high, width_low], 1),
            jnp.concatenate([width_high, width_low], 1),
        ],
        0,
    )

    def load(quad):
        return jnp.concatenate(
            [
                held[row * col_count + quad // pairs, quad % pairs]
                for row in range(row_count)
            ],
            0,
        )

    @pl.loop(0, quads // 2, unroll=2)
    def _(step):
        both = jnp.concatenate([load(2 * step), load(2 * step + 1)], 1)
        high, low = split(both)
        conv = dot(time_stack, jnp.concatenate([high, low], 0))
        conv = conv[:frames] + conv[frames:]
        conv = jnp.concatenate([conv[:, :LANES], conv[:, LANES:]], 0)
        high, low = split(conv)
        conv = dot(jnp.concatenate([high, low], 1), width_stack)
        conv = conv[:, :LANES] + conv[:, LANES:]
        work[pl.ds(2 * pitch * step, frames), :] = conv[:frames]
        work[pl.ds(2 * pitch * step + pitch, frames), :] = conv[frames:]

    height_stack = jnp.concatenate(
        [left_stack(shifted_rows(taps[2 + e : 3 + e], quads)[:, :quads]) for e in range(3)], 0
    )
    group = 4
    lane = lax.broadcasted_iota(jnp.int32, (quads, group * LANES), 1) % LANES

    @pl.loop(0, frames // group, unroll=2)
    def _(step):
        tiles = [
            work[pl.ds(group * step + e, quads, stride=pitch), :] for e in range(group)
        ]
        high, low = split(jnp.concatenate(tiles, 1))
        conv = dot(height_stack, jnp.concatenate([high, low], 0))
        same = conv[:quads] + conv[quads : 2 * quads]
        upper = conv[2 * quads : 3 * quads] + conv[3 * quads : 4 * quads]
        lower = conv[4 * quads : 5 * quads] + conv[5 * quads :]
        cross = jnp.where(lane < width, upper, lower)
        for e in range(group):
            cols = slice(e * LANES, (e + 1) * LANES)
            work[pl.ds(group * step + e, quads, stride=pitch), :] = same[:, cols] + pltpu.roll(
                cross[:, cols], width, 1
            )

    gain = taps[5:6]
    for place in range(devices):
        other = me_ref[0] ^ place
        row, col = other // col_count, other % col_count
        for pair in range(pairs):
            start = (col * pairs + pair) * pitch + row * frame_rows
            value = work[pl.ds(start, frame_rows), :]
            value = value + gain * src_refs[place][0, pair]
            value = 0.5 * value * (1.0 + lax.erf(value * math.sqrt(0.5)))
            dst_refs[place][0, pair] = value


def conv_chunk(packed, me, taps, row_count, col_count):
    devices = len(packed)
    share, pairs, frame_rows, _ = packed[0].shape
    frames = row_count * frame_rows
    quads = col_count * pairs
    pack = 2
    block = pl.BlockSpec((1, pairs, frame_rows, LANES), lambda i, me: (i, 0, 0, 0))
    cells = frames * quads * LANES
    return pl.pallas_call(
        functools.partial(conv_kernel, (row_count, col_count, pairs, frame_rows, pack)),
        grid_spec=pltpu.PrefetchScalarGridSpec(
            num_scalar_prefetch=1,
            grid=(share,),
            in_specs=[pl.BlockSpec((1, SUBLANES, LANES), lambda i, me: (i, 0, 0))]
            + [block] * devices,
            out_specs=[block] * devices,
            scratch_shapes=[
                pltpu.VMEM((devices, pairs, frame_rows, LANES), jnp.float32),
                pltpu.VMEM((quads * (frames + 1), LANES), jnp.float32),
            ],
        ),
        out_shape=[jax.ShapeDtypeStruct(packed[0].shape, jnp.float32)] * devices,
        cost_estimate=pl.CostEstimate(
            flops=share * cells * 2000, transcendentals=share * cells, bytes_accessed=8 * share * cells
        ),
        name="conv",
    )(me, taps, *packed)


def on_device(
    video, decay_rates, frequencies, input_vec, output_vec, lowrank_vec, step_scale, skip_gain
):
    clip_count, frame_rows, height_rows, width_cells, channels = video.shape
    row_count = lax.axis_size("row")
    col_count = lax.axis_size("col")
    frames = frame_rows * row_count
    height = height_rows * col_count
    dev_count = row_count * col_count
    pack = LANES // width_cells
    pairs = height_rows // pack
    chunk_width = channels // CHUNKS
    share = chunk_width // dev_count
    assert clip_count == 1 and pack == 2 and chunk_width == LANES and frames == LANES
    me = lax.axis_index("row") * col_count + lax.axis_index("col")
    shape = video.shape[1:]
    video = video.reshape(shape)

    def own(array, dim):
        split_shape = array.shape[:dim] + (CHUNKS, chunk_width) + array.shape[dim + 1 :]
        part = lax.dynamic_slice_in_dim(array.reshape(split_shape), me * share, share, dim + 1)
        return part.reshape(array.shape[:dim] + (CHUNKS * share,) + array.shape[dim + 1 :])

    me_arg = me.reshape(1).astype(jnp.int32)

    def exchange(blocks, name):
        if dev_count > MOST_PERMUTES:
            turn = jnp.arange(dev_count, dtype=jnp.int32) ^ me
            whole = lax.all_to_all(jnp.stack(blocks)[turn], ("row", "col"), 0, 0, tiled=True)
            return list(whole[turn])
        moved = list(blocks)
        for place in range(1, dev_count):
            with jax.named_scope(f"{name}_{place}"):
                pairs_of = [(e, e ^ place) for e in range(dev_count)]
                moved[place] = lax.ppermute(blocks[place], ("row", "col"), pairs_of)
        return moved

    packed = [pack_chunk(video, me_arg, chunk, pack, dev_count) for chunk in range(CHUNKS)]
    packed = [exchange(packed[chunk], f"in{chunk}") for chunk in range(CHUNKS)]

    decay_rates, frequencies = own(decay_rates, 1), own(frequencies, 1)
    input_vec, output_vec, lowrank_vec = own(input_vec, 2), own(output_vec, 2), own(lowrank_vec, 2)
    step_scale, gains = own(step_scale, 1), own(skip_gain, 0)
    lane = jnp.arange(LANES, dtype=jnp.int32)
    lags = (
        -lane,
        jnp.concatenate([-pack * lane, 1 - pack * lane, -1 - pack * lane]),
        lane,
    )
    time_rows, height_rows_taps, width_rows = (
        axis_rows(
            decay_rates[axis],
            frequencies[axis],
            input_vec[axis],
            output_vec[axis],
            lowrank_vec[axis],
            step_scale[axis],
            length,
            lags[axis],
        )
        for axis, length in enumerate((frames, height, width_cells))
    )
    own_count = CHUNKS * share
    taps = jnp.concatenate(
        [
            time_rows[:, None],
            width_rows[:, None],
            height_rows_taps.reshape(own_count, 3, LANES),
            jnp.broadcast_to(gains[:, None, None], (own_count, SUBLANES - 5, LANES)),
        ],
        1,
    ).reshape(CHUNKS, share, SUBLANES, LANES)

    outs = []
    for chunk in range(CHUNKS):
        outs.append(conv_chunk(packed[chunk], me_arg, taps[chunk], row_count, col_count))
    outs = [exchange(outs[chunk], f"out{chunk}") for chunk in range(CHUNKS)]
    result = None
    for chunk in range(CHUNKS):
        result = unpack_chunk(outs[chunk], me_arg, chunk, pack, shape, result)
    return result.reshape((clip_count,) + shape)


def solution(mesh):
    in_specs = (P(None, "row", "col", None, None), P(), P(), P(), P(), P(), P(), P())
    out_specs = P(None, "row", "col", None, None)
    return jax.shard_map(
        on_device, mesh=mesh, in_specs=in_specs, out_specs=out_specs, check_vma=False
    )
```
